256 devices in a mesh: dp: 16 (over x_lo, y, core), tensor: 16 (over z, x_hi).
Axes of the slice: x: 4 (x_hi: 2, x_lo: 2; x = x_hi * 2 + x_lo), y: 4, z: 8, core: 2. Of those that a mesh axis runs over, the one named last changes fastest.
Arguments:
- target_hidden: bfloat16 [512, 16384], P('dp', 'tensor'), may hold values from -64 to 64
- target_gain: bfloat16 [16384], replicated, may hold values from 0.25 to 1.75
- target_head: bfloat16 [16384, 65536], P(None, ('dp', 'tensor')), may hold values from -8 to 8
- reference_hidden: bfloat16 [512, 4096], P('dp', 'tensor'), may hold values from -64 to 64
- reference_gain: bfloat16 [4096], replicated, may hold values from 0.25 to 1.75
- reference_head: bfloat16 [4096, 65536], P(None, ('dp', 'tensor')), may hold values from -8 to 8
Outputs:
- contrast: float32 [512, 65536], P(None, ('dp', 'tensor'))
The draws below stay inside these ranges and needn't reach their ends.
All inputs are finite; a program needn't handle non-finite values.
Results may differ from the reference program's by a relative error of at most 0.0012.
Values may be sent and summed in bfloat16 or wider, within the bound.
No kernel may reach another device: no remote copies, remote signals or barrier semaphores. Data moves between devices by JAX's collectives and lax.ppermute only.
A program may use at most 128 MiB of HBM per device.

```python
import jax
import jax.numpy as jnp
from jax import lax

ROWS = 512
D = 16384
DR = 4096
V = 65536


def head_matrix(key, width, columns):

    def one_column(column):
        column_key = jax.random.fold_in(key, column)
        values = jnp.clip(jax.random.normal(column_key, (width,), jnp.float32), -6.0, 6.0)
        wobble = jax.random.uniform(jax.random.fold_in(column_key, 7), (), jnp.float32, -0.3, 0.3)
        factor = 3.0 * jnp.exp2(column.astype(jnp.float32) / V) * jnp.exp(wobble)
        return values * factor / jnp.sqrt(jnp.float32(width))
    return jnp.clip(jax.vmap(one_column)(columns).T, -8.0, 8.0)


def hidden_rows(key, width, count):
    keys = jax.random.split(key, 2)
    column_scale = jnp.power(10.0, jnp.arange(width, dtype=jnp.float32) / width)[None, :]
    row_scale = jnp.power(10.0, jax.random.uniform(keys[1], (count, 1), jnp.float32))
    base = jnp.clip(jax.random.normal(keys[0], (count, width), jnp.float32), -6.0, 6.0)
    values = 0.2 * base * row_scale * column_scale
    return jnp.clip(values, -64.0, 64.0)


def draw_target_head(key, part):
    return head_matrix(jax.random.fold_in(key, 21), D, jnp.arange(V)).astype(jnp.bfloat16)


def draw_reference_head(key, part):
    return head_matrix(jax.random.fold_in(key, 31), DR, jnp.arange(V)).astype(jnp.bfloat16)


def draw_target_hidden(key, part):
    return hidden_rows(jax.random.fold_in(key, 22), D, ROWS).astype(jnp.bfloat16)


def draw_reference_hidden(key, part):
    return hidden_rows(jax.random.fold_in(key, 32), DR, ROWS).astype(jnp.bfloat16)


def setup_inputs(seed: int = 0) -> dict:
    key_list = jax.random.split(jax.random.key(seed), 7)
    return {
        "target_hidden": draw_target_hidden(jax.random.fold_in(key_list[6], 71), 0),
        "target_gain": jnp.clip(1.0 + 0.15 * jax.random.normal(key_list[1], (D,), jnp.float32), 0.25, 1.75).astype(jnp.bfloat16),
        "target_head": draw_target_head(jax.random.fold_in(key_list[6], 71), 0),
        "reference_hidden": draw_reference_hidden(jax.random.fold_in(key_list[6], 71), 0),
        "reference_gain": jnp.clip(1.0 + 0.15 * jax.random.normal(key_list[4], (DR,), jnp.float32), 0.25, 1.75).astype(jnp.bfloat16),
        "reference_head": draw_reference_head(jax.random.fold_in(key_list[6], 71), 0),
    }


EPS = 1e-05
LOG_TEN = 2.302585092994046

def model_parts(hidden, gain, head):
    values = hidden.astype(jnp.float32)
    square_mean = lax.optimization_barrier(jnp.mean(values * values, axis=1, keepdims=True))
    normed = (values * lax.rsqrt(square_mean + EPS) * gain.astype(jnp.float32)).astype(jnp.bfloat16)
    logits = jnp.dot(normed, head, preferred_element_type=jnp.float32)
    peak = lax.optimization_barrier(jnp.max(logits, axis=1, keepdims=True))
    total = lax.optimization_barrier(jnp.sum(jnp.exp(logits - peak), axis=1, keepdims=True))
    return (logits, peak, peak + jnp.log(total))

def reference(target_hidden, target_gain, target_head, reference_hidden, reference_gain, reference_head):
    target_logits, target_peak, target_lse = model_parts(target_hidden, target_gain, target_head)
    reference_logits, reference_peak, reference_lse = model_parts(reference_hidden, reference_gain, reference_head)
    margin = jnp.minimum(0.0, target_logits - target_peak + LOG_TEN)
    return target_logits - target_lse - 0.5 * (reference_logits - reference_lse) + margin
```

```python
import functools

import jax
import jax.numpy as jnp
import numpy as np
from jax import lax
from jax.experimental import pallas as pl
from jax.experimental.pallas import tpu as pltpu
from jax.sharding import Mesh
from jax.sharding import PartitionSpec as P

EPS = 1e-05
LOG_TEN = 2.302585092994046

AXES = ("xl", "y", "core", "z", "xh")
SIZES = (2, 4, 2, 8, 2)
NX, NY, NZ = 4, 4, 8

D, DR = 16384, 4096
ROWS = 256
COLS = 256
GROUP = 32
WT, WR = 1024, 256
FA = 768
FC = WT - FA + WR
RING4 = (0, -1, 1, 2)
RING8 = (0, -1, 1, -2, 2, -3, 3, 4)


def flat_index(x, y, z, c):
    xl, xh = x % 2, x // 2
    return (((xl * NY + y) * 2 + c) * NZ + z) * 2 + xh


def permutation(move):
    pairs = []
    for x in range(NX):
        for y in range(NY):
            for z in range(NZ):
                for c in range(2):
                    dx, dy, dz, dc = move(c)
                    to = flat_index((x + dx) % NX, (y + dy) % NY, (z + dz) % NZ, (c + dc) % 2)
                    pairs.append((flat_index(x, y, z, c), to))
    return sorted(pairs)


def send(value, move):
    return lax.ppermute(value, AXES, permutation(move))


def along_z(step):
    return lambda c: (0, 0, step, 0)


def along_x(step):
    return lambda c: (step, 0, 0, 0)


def along_y(step):
    return lambda c: (0, step, 0, 0)


def other_core(c):
    return (0, 0, 0, 1)


def x_or_y(step, x_core):
    return lambda c: (step, 0, 0, 0) if c == x_core else (0, step, 0, 0)


def ring4(value, x_core):
    low = send(value, x_or_y(1, x_core))
    high = send(value, x_or_y(-1, x_core))
    far = send(low, x_or_y(1, x_core))
    return [value, low, high, far]


def ring8(value, core):
    low1 = send(value, along_z(1))
    high1 = send(value, along_z(-1))
    low2 = send(low1, along_z(1))
    high2 = send(high1, along_z(-1))
    low3 = send(low2, along_z(1))
    high3 = send(high2, along_z(-1))
    far = send(jnp.where(core == 0, low3, high3), lambda c: (0, 0, 1 if c == 0 else -1, 0))
    return [value, low1, high1, low2, high2, low3, high3, far]


def squares(values):
    wide = values.astype(jnp.float32)
    return wide * wide


def heads_kernel(
    table_ref,
    ss_a0, ss_a1, ss_a2, ss_a3, ss_a4, ss_ct, ss_cr,
    gain_t_ref, gain_r_ref,
    a0, a1, a2, a3, a4,
    c0, c1, c2, c3, c4, c5, c6, c7,
    head_t_own, head_t_other, head_r_own, head_r_other,
    logits_t_own, logits_t_other, logits_r_own, logits_r_other, stats_ref,
    buf_a, buf_c, buf_t, buf_r, scale_t, scale_r, left_t, left_r, sems,
):
    a_refs = (a0, a1, a2, a3, a4)
    a_slots = ((0, 0, 4), (1, 0, 4), (2, 0, 4), (3, 0, 2), (3, 2, 2))
    c_refs = (c0, c1, c2, c3, c4, c5, c6, c7)

    def copies(i):
        out = []
        for n, (ref, (k, j, count)) in enumerate(zip(a_refs, a_slots)):
            out.append(
                pltpu.make_async_copy(ref.at[:, i], buf_a.at[i, k, pl.ds(j, count)], sems.at[i, n])
            )
        out.append(pltpu.make_async_copy(c_refs[i], buf_c.at[i], sems.at[i, 5]))
        z = table_ref[32 + i]
        for n, (ref, slot) in enumerate(((head_t_own, 0), (head_t_other, 1))):
            out.append(pltpu.make_async_copy(ref.at[z], buf_t.at[i, slot], sems.at[i, 6 + n]))
        for n, (ref, slot) in enumerate(((head_r_own, 0), (head_r_other, 1))):
            out.append(pltpu.make_async_copy(ref.at[z], buf_r.at[i, slot], sems.at[i, 8 + n]))
        return out

    for i in range(NZ):
        for copy in copies(i):
            copy.start()

    scale_t[...] = jnp.zeros_like(scale_t)
    scale_r[...] = jnp.zeros_like(scale_r)
    for ref, (k, j, count) in zip((ss_a0, ss_a1, ss_a2, ss_a3, ss_a4), a_slots):
        for n in range(count):
            group = table_ref[k * 4 + j + n]
            scale_t[group] += ref[n]
    for n in range(16):
        group = table_ref[40 + n]
        scale_t[group] += ss_ct[n]
        scale_r[group] += ss_cr[n]
    scale_t[...] = lax.rsqrt(scale_t[...] * (1.0 / D) + EPS)
    scale_r[...] = lax.rsqrt(scale_r[...] * (1.0 / DR) + EPS)

    for i in range(NZ):
        for copy in copies(i):
            copy.wait()
        z = table_ref[32 + i]
        gains_t = [gain_t_ref[z * 2 + h] for h in range(2)]
        gains_r = [gain_r_ref[z * 2 + h] for h in range(2)]

        def place_a(n, carry):
            group, xh = table_ref[n], table_ref[16 + n]
            gain = gain_t_ref[z * 2 + xh][:, :FA]
            values = buf_a[i, n // 4, n % 4].astype(jnp.float32)
            rows = pl.ds(pl.multiple_of(group * GROUP, GROUP), GROUP)
            left_t[xh, rows, :FA] = (values * scale_t[group] * gain).astype(jnp.bfloat16)
            return carry

        def place_c(n, carry):
            group, xh = table_ref[40 + n], table_ref[56 + n]
            gain_t = gain_t_ref[z * 2 + xh][:, FA:]
            gain_r = gain_r_ref[z * 2 + xh]
            values = buf_c[i, n].astype(jnp.float32)
            rows = pl.ds(pl.multiple_of(group * GROUP, GROUP), GROUP)
            part_t = values[:, : WT - FA] * scale_t[group] * gain_t
            part_r = values[:, WT - FA :] * scale_r[group] * gain_r
            left_t[xh, rows, FA:] = part_t.astype(jnp.bfloat16)
            left_r[xh, rows, :] = part_r.astype(jnp.bfloat16)
            return carry

        lax.fori_loop(0, 16, place_a, 0)
        lax.fori_loop(0, 16, place_c, 0)
        outs = ((logits_t_own, logits_r_own), (logits_t_other, logits_r_other))
        for slot in range(2):
            out_t, out_r = outs[slot]
            sum_t = sum(
                jnp.dot(left_t[h], buf_t[i, slot, h], preferred_element_type=jnp.float32)
                for h in range(2)
            )
            sum_r = sum(
                jnp.dot(left_r[h], buf_r[i, slot, h], preferred_element_type=jnp.float32)
                for h in range(2)
            )
            if i == 0:
                out_t[...] = sum_t
                out_r[...] = sum_r
            else:
                out_t[...] += sum_t
                out_r[...] += sum_r

    columns = []
    for own, other in ((logits_t_own, logits_t_other), (logits_r_own, logits_r_other)):
        one, two = own[...], other[...]
        peak = jnp.max(jnp.maximum(one, two), axis=1, keepdims=True)
        total = jnp.sum(jnp.exp(one - peak) + jnp.exp(two - peak), axis=1, keepdims=True)
        columns.append((peak, total))
    lane = lax.broadcasted_iota(jnp.int32, (ROWS, 128), 1)
    packed = jnp.where(
        lane == 0,
        columns[0][0],
        jnp.where(lane == 1, columns[1][0], jnp.where(lane == 2, columns[0][1], columns[1][1])),
    )
    stats_ref[...] = packed.T[:8, :]


def contrast_kernel(core_ref, own_ref, other_ref, t_own, r_own, t_other, r_other, out_ref):
    core = core_ref[0]

    def score(stats, logits_t, logits_r, where):
        tall = jnp.concatenate([stats, jnp.zeros((120, ROWS), jnp.float32)], axis=0).T
        peak_t, peak_r = tall[:, 0:1], tall[:, 1:2]
        lse_t = peak_t + jnp.log(tall[:, 2:3])
        lse_r = peak_r + jnp.log(tall[:, 3:4])
        margin = jnp.minimum(0.0, logits_t - peak_t + LOG_TEN)
        value = logits_t - lse_t - 0.5 * (logits_r - lse_r) + margin
        for group in range(ROWS // GROUP):
            out_ref[group, where] = value[group * GROUP : (group + 1) * GROUP]

    score(own_ref[...], t_own[...], r_own[...], core)
    score(other_ref[...], t_other[...], r_other[...], 1 - core)


def merge(parts):
    peaks = functools.reduce(jnp.maximum, [p[0:2] for p in parts])
    totals = sum(p[2:4] * jnp.exp(p[0:2] - peaks) for p in parts)
    return jnp.concatenate([peaks, totals, jnp.zeros_like(p8(parts[0]))], axis=0)


def p8(part):
    return part[4:8]


def local(hidden_t, gain_t, head_t, hidden_r, gain_r, head_r):
    xl, y, core, z, xh = (lax.axis_index(name) for name in AXES)
    x = 2 * xh + xl

    head_t_other = send(head_t, other_core)
    head_r_other = send(head_r, other_core)

    part_a = hidden_t[:, :FA]
    part_c = jnp.concatenate([hidden_t[:, FA:], hidden_r], axis=1)

    first_c = jnp.stack(ring4(part_c, 0))
    second_c = jnp.stack(ring4(first_c, 1)).reshape(16, GROUP, FC)
    first_a = jnp.stack(ring8(part_a, core))
    second_a = jnp.stack(ring4(first_a, 1))
    blocks_c = ring8(second_c, core)
    low = send(second_a, x_or_y(1, 0))
    high = send(second_a, x_or_y(-1, 0))
    far_low = send(low[:2], x_or_y(1, 0))
    far_high = send(high[2:], x_or_y(-1, 0))
    blocks_a = [second_a, low, high, far_low, far_high]

    ss_a = [jnp.sum(squares(b), axis=(1, 3))[:, :, None] for b in blocks_a]
    ss_ct = sum(jnp.sum(squares(b[:, :, : WT - FA]), axis=2) for b in blocks_c)[:, :, None]
    ss_cr = sum(jnp.sum(squares(b[:, :, WT - FA :]), axis=2) for b in blocks_c)[:, :, None]

    ring = jnp.array(RING4, jnp.int32)
    last, first = ring[:, None] + jnp.zeros((4, 4), jnp.int32), ring[None, :] + jnp.zeros((4, 4), jnp.int32)
    on_x = core == 0
    xa = (x + jnp.where(on_x, last, first)) % NX
    ya = (y + jnp.where(on_x, first, last)) % NY
    xc = (x + jnp.where(on_x, first, last)) % NX
    yc = (y + jnp.where(on_x, last, first)) % NY
    zs = (z + jnp.array(RING8, jnp.int32)) % NZ
    table = jnp.concatenate(
        [
            ((xa % 2) * NY + ya).reshape(16),
            (xa // 2).reshape(16),
            zs,
            ((xc % 2) * NY + yc).reshape(16),
            (xc // 2).reshape(16),
        ]
    ).astype(jnp.int32)

    wide_gain_t = gain_t.astype(jnp.float32).reshape(16, 1, WT)
    wide_gain_r = gain_r.astype(jnp.float32).reshape(16, 1, WR)
    vmem = pl.BlockSpec(memory_space=pltpu.VMEM)
    smem = pl.BlockSpec(memory_space=pltpu.SMEM)
    hbm = pl.BlockSpec(memory_space=pl.ANY)
    square = jax.ShapeDtypeStruct((ROWS, COLS), jnp.float32)
    bf16 = jnp.bfloat16
    t_own, t_cross, r_own, r_cross, stats = pl.pallas_call(
        heads_kernel,
        out_shape=[square] * 4 + [jax.ShapeDtypeStruct((8, ROWS), jnp.float32)],
        in_specs=[smem] + [vmem] * 9 + [hbm] * 17,
        out_specs=[vmem] * 5,
        scratch_shapes=[
            pltpu.VMEM((NZ, 4, 4, GROUP, FA), bf16),
            pltpu.VMEM((NZ, 16, GROUP, FC), bf16),
            pltpu.VMEM((NZ, 2, 2, WT, COLS), bf16),
            pltpu.VMEM((NZ, 2, 2, WR, COLS), bf16),
            pltpu.VMEM((8, GROUP, 1), jnp.float32),
            pltpu.VMEM((8, GROUP, 1), jnp.float32),
            pltpu.VMEM((2, ROWS, WT), bf16),
            pltpu.VMEM((2, ROWS, WR), bf16),
            pltpu.SemaphoreType.DMA((NZ, 10)),
        ],
        compiler_params=pltpu.CompilerParams(vmem_limit_bytes=52 * 2**20),
        name="heads",
    )(
        table,
        *ss_a, ss_ct, ss_cr,
        wide_gain_t, wide_gain_r,
        *blocks_a, *blocks_c,
        head_t.reshape(NZ, 2, WT, COLS), head_t_other.reshape(NZ, 2, WT, COLS),
        head_r.reshape(NZ, 2, WR, COLS), head_r_other.reshape(NZ, 2, WR, COLS),
    )

    t_other = send(t_cross, other_core)
    r_other = send(r_cross, other_core)
    stats = merge([stats] + [send(stats, along_x(s)) for s in (1, -1, 2)])
    stats = merge([stats] + [send(stats, along_y(s)) for s in (1, -1, 2)])
    stats = merge([stats] + [send(stats, along_z(s)) for s in (2, -2, 4)])
    stats = merge([stats, send(stats, along_z(1))])
    stats_other = send(stats, other_core)

    out = pl.pallas_call(
        contrast_kernel,
        out_shape=jax.ShapeDtypeStruct((8, 2, GROUP, COLS), jnp.float32),
        in_specs=[smem] + [vmem] * 6,
        out_specs=vmem,
        name="contrast",
    )(core.astype(jnp.int32).reshape(1), stats, stats_other, t_own, r_own, t_other, r_other)
    return out.reshape(2 * ROWS, COLS)


def solution(mesh):
    fine = Mesh(np.asarray(mesh.devices).reshape(SIZES), AXES)
    rows, features, vocabulary = ("xl", "y", "core"), ("z", "xh"), AXES
    placed = (
        P(rows, features),
        P(),
        P(None, vocabulary),
        P(rows, features),
        P(),
        P(None, vocabulary),
    )
    return jax.shard_map(
        local, mesh=fine, in_specs=placed, out_specs=P(None, vocabulary), check_vma=False
    )
```

```python
import functools

import jax
import jax.numpy as jnp
import numpy as np
from jax import lax
from jax.experimental import pallas as pl
from jax.experimental.pallas import tpu as pltpu
from jax.sharding import Mesh
from jax.sharding import PartitionSpec as P

EPS = 1e-05
LOG_TEN = 2.302585092994046

AXES = ("xl", "y", "core", "z", "xh")
SIZES = (2, 4, 2, 8, 2)
NX, NY, NZ = 4, 4, 8

D, DR = 16384, 4096
ROWS = 256
COLS = 256
GROUP = 32
WT, WR = 1024, 256
FA = 896
FC = WT - FA + WR
RING8 = (0, -1, 1, -2, 2, -3, 3, 4)


def flat_index(x, y, z, c):
    xl, xh = x % 2, x // 2
    return (((xl * NY + y) * 2 + c) * NZ + z) * 2 + xh


def send(value, move):
    pairs = []
    for xl, y, c, z, xh in np.ndindex(*SIZES):
        x = 2 * xh + xl
        tx, ty, tz, tc = move(x, y, z, c)
        pairs.append((flat_index(x, y, z, c), flat_index(tx % NX, ty % NY, tz % NZ, tc % 2)))
    return lax.ppermute(value, AXES, pairs)


PAIRS4 = ((1, 0, 3, 2), (3, 2, 1, 0))
PAIRS8 = ((1, 0, 3, 2, 5, 4, 7, 6), (7, 2, 1, 4, 3, 6, 5, 0), (3, 6, 5, 0, 7, 2, 1, 4))


def sources(pairs):
    rows = [[place] for place in range(len(pairs[0]))]
    for partner in pairs:
        rows = [rows[place] + rows[partner[place]] for place in range(len(rows))]
    return np.array(rows, np.int32)


def along_z(step):
    return lambda x, y, z, c: (x, y, z + step, c)


def pair_z(partner):
    return lambda x, y, z, c: (x, y, partner[z], c)


def pair_x(partner):
    return lambda x, y, z, c: (partner[x], y, z, c)


def pair_y(partner):
    return lambda x, y, z, c: (x, partner[y], z, c)


def pair_x_or_y(partner, x_core):
    return lambda x, y, z, c: (partner[x], y, z, c) if c == x_core else (x, partner[y], z, c)


def other_core(x, y, z, c):
    return (x, y, z, 1 - c)


def x_or_y(step, x_core):
    return lambda x, y, z, c: (x + step, y, z, c) if c == x_core else (x, y + step, z, c)


def after(value, *others):
    return lax.optimization_barrier((value,) + others)[0]


def ring8(value, core):
    low1 = send(value, along_z(1))
    high1 = send(value, along_z(-1))
    low2 = send(low1, along_z(1))
    high2 = send(high1, along_z(-1))
    low3 = send(low2, along_z(1))
    high3 = send(high2, along_z(-1))
    far = send(jnp.where(core == 0, low3, high3), lambda x, y, z, c: (x, y, z + 1 - 2 * c, c))
    return [value, low1, high1, low2, high2, low3, high3, far]


A_SLOTS = ((0, 0, 2), (0, 2, 2), (1, 0, 2), (1, 2, 2), (2, 0, 2), (2, 2, 2), (3, 0, 2), (3, 2, 2))
NA = len(A_SLOTS)
AHEAD = 2


def heads_kernel(*refs):
    table_ref, gain_t_ref, gain_r_ref = refs[:3]
    a_refs, c_refs, head_refs = refs[3 : 3 + NA], refs[3 + NA : 11 + NA], refs[11 + NA : 15 + NA]
    head_t_own, head_t_other, head_r_own, head_r_other = head_refs
    logits_own, logits_cross, stats_ref = refs[15 + NA : 18 + NA]
    buf_a, buf_c, buf_t, buf_r = refs[18 + NA : 22 + NA]
    scale_t, scale_r, sums, left_t0, left_r0, left_t1, left_r1, sum_t, sum_r, sem_x, sem_h = refs[22 + NA :]
    lefts = ((left_t0, left_r0), (left_t1, left_r1))

    def hidden_copies(i, c_ref):
        out = []
        place_a = table_ref[72 + i]
        for n, (ref, (k, j, count)) in enumerate(zip(a_refs, A_SLOTS)):
            target = buf_a.at[i, k, pl.ds(j, count)]
            out.append(pltpu.make_async_copy(ref.at[:, place_a], target, sem_x.at[i, n]))
        out.append(pltpu.make_async_copy(c_ref, buf_c.at[i], sem_x.at[i, NA]))
        return out

    def head_copies(i):
        z = table_ref[32 + i]
        own, other = pl.ds(0, COLS), pl.ds(COLS, COLS)
        return [
            pltpu.make_async_copy(head_t_own.at[z], buf_t.at[i, :, own], sem_h.at[i, 0]),
            pltpu.make_async_copy(head_t_other.at[z], buf_t.at[i, :, other], sem_h.at[i, 1]),
            pltpu.make_async_copy(head_r_own.at[z], buf_r.at[i, :, own], sem_h.at[i, 2]),
            pltpu.make_async_copy(head_r_other.at[z], buf_r.at[i, :, other], sem_h.at[i, 3]),
        ]

    for i in range(NZ):
        for copy in hidden_copies(i, c_refs[i]):
            copy.start()
    def start_heads(i):
        for copy in head_copies(i):
            copy.start()

    for i in range(AHEAD):
        start_heads(i)

    sums[...] = jnp.zeros_like(sums)

    def square_step(i, carry):
        for copy in hidden_copies(i, c_refs[0]):
            copy.wait()

        def lanes(ref, low, high):
            total = None
            for at in range(low, high, 128):
                part = ref[:, at : at + 128].astype(jnp.float32)
                total = part * part if total is None else total + part * part
            return total

        for n in range(16):
            sums[0, n] += lanes(buf_a.at[i, n // 4, n % 4], 0, FA)
            sums[1, n] += lanes(buf_c.at[i, n], 0, WT - FA)
            sums[2, n] += lanes(buf_c.at[i, n], WT - FA, FC)
        return carry

    lax.fori_loop(0, NZ, square_step, 0)
    scale_t[...] = jnp.zeros_like(scale_t)
    scale_r[...] = jnp.zeros_like(scale_r)
    for n in range(16):
        scale_t[table_ref[n]] += sums[0, n]
        scale_t[table_ref[40 + n]] += sums[1, n]
        scale_r[table_ref[40 + n]] += sums[2, n]
    for scale, width in ((scale_t, D), (scale_r, DR)):
        mean = jnp.sum(scale[...], axis=2, keepdims=True) * (1.0 / width)
        scale[...] = jnp.broadcast_to(lax.rsqrt(mean + EPS), scale.shape)

    def place(i, left):
        left_t, left_r = left
        z = table_ref[32 + i]

        def put(source, at, scale, group, gain, target, xh, column, width):
            rows = pl.ds(pl.multiple_of(group * GROUP, GROUP), GROUP)
            value = source[:, at : at + 128].astype(jnp.float32)
            value = value * scale[group] * gain[z * 2 + xh][:, column : column + 128]
            to = pl.ds(pl.multiple_of(xh * width + column, 128), 128)
            target[rows, to] = value.astype(jnp.bfloat16)

        for n in range(16):
            group, xh = table_ref[n], table_ref[16 + n]
            for at in range(0, FA, 128):
                put(buf_a.at[i, n // 4, n % 4], at, scale_t, group, gain_t_ref, left_t, xh, at, WT)
            group, xh = table_ref[40 + n], table_ref[56 + n]
            for at in range(0, WT - FA, 128):
                put(buf_c.at[i, n], at, scale_t, group, gain_t_ref, left_t, xh, FA + at, WT)
            for at in range(0, WR, 128):
                source = buf_c.at[i, n]
                put(source, WT - FA + at, scale_r, group, gain_r_ref, left_r, xh, at, WR)

    sum_t[...] = jnp.zeros_like(sum_t)
    sum_r[...] = jnp.zeros_like(sum_r)

    def multiply(i, left):
        left_t, left_r = left
        sum_t[...] += jnp.dot(left_t[...], buf_t[i], preferred_element_type=jnp.float32)
        sum_r[...] += jnp.dot(left_r[...], buf_r[i], preferred_element_type=jnp.float32)

    def wait_heads(i):
        for copy in head_copies(i):
            copy.wait()

    place(0, lefts[0])

    def pair_step(pair, carry):
        i = pair * 2
        wait_heads(i)

        @pl.when(i + AHEAD < NZ)
        def _():
            start_heads(i + AHEAD)

        place(i + 1, lefts[1])
        multiply(i, lefts[0])
        wait_heads(i + 1)

        @pl.when(i + 1 + AHEAD < NZ)
        def _():
            start_heads(i + 1 + AHEAD)

        place(jnp.minimum(i + 2, NZ - 1), lefts[0])
        multiply(i + 1, lefts[1])
        return carry

    lax.fori_loop(0, NZ // 2, pair_step, 0)
    for model, total in enumerate((sum_t, sum_r)):
        logits_own[model] = total[:, :COLS]
        logits_cross[model] = total[:, COLS:]

    columns = []
    for model in range(2):
        one, two = logits_own[model], logits_cross[model]
        peak = jnp.max(jnp.maximum(one, two), axis=1, keepdims=True)
        total = jnp.sum(jnp.exp(one - peak) + jnp.exp(two - peak), axis=1, keepdims=True)
        columns.append((peak, total))
    lane = lax.broadcasted_iota(jnp.int32, (ROWS, 128), 1)
    packed = jnp.where(
        lane == 0,
        columns[0][0],
        jnp.where(lane == 1, columns[1][0], jnp.where(lane == 2, columns[0][1], columns[1][1])),
    )
    stats_ref[...] = packed.T[:8, :]


def contrast_kernel(core_ref, own_ref, other_ref, logits_own, logits_other, out_ref):
    core = core_ref[0]

    def score(stats, logits, where):
        logits_t, logits_r = logits[0], logits[1]
        tall = jnp.concatenate([stats, jnp.zeros((120, ROWS), jnp.float32)], axis=0).T
        peak_t, peak_r = tall[:, 0:1], tall[:, 1:2]
        lse_t = peak_t + jnp.log(tall[:, 2:3])
        lse_r = peak_r + jnp.log(tall[:, 3:4])
        margin = jnp.minimum(0.0, logits_t - peak_t + LOG_TEN)
        value = logits_t - lse_t - 0.5 * (logits_r - lse_r) + margin
        for group in range(ROWS // GROUP):
            out_ref[group, where] = value[group * GROUP : (group + 1) * GROUP]

    score(own_ref[...], logits_own, core)
    score(other_ref[...], logits_other, 1 - core)


def merge(parts):
    peaks = functools.reduce(jnp.maximum, [p[0:2] for p in parts])
    totals = sum(p[2:4] * jnp.exp(p[0:2] - peaks) for p in parts)
    return jnp.concatenate([peaks, totals, jnp.zeros_like(p8(parts[0]))], axis=0)


def p8(part):
    return part[4:8]


vmem = pl.BlockSpec(memory_space=pltpu.VMEM)
smem = pl.BlockSpec(memory_space=pltpu.SMEM)
hbm = pl.BlockSpec(memory_space=pl.ANY)


def heads_call(*operands):
    square = jax.ShapeDtypeStruct((2, ROWS, COLS), jnp.float32)
    bf16 = jnp.bfloat16
    return pl.pallas_call(
        heads_kernel,
        out_shape=[square] * 2 + [jax.ShapeDtypeStruct((8, ROWS), jnp.float32)],
        in_specs=[smem] + [vmem] * 2 + [hbm] * (NA + 12),
        out_specs=[vmem] * 3,
        scratch_shapes=[
            pltpu.VMEM((NZ, 4, 4, GROUP, FA), bf16),
            pltpu.VMEM((NZ, 16, GROUP, FC), bf16),
            pltpu.VMEM((NZ, 2 * WT, 2 * COLS), bf16),
            pltpu.VMEM((NZ, 2 * WR, 2 * COLS), bf16),
            pltpu.VMEM((8, GROUP, 128), jnp.float32),
            pltpu.VMEM((8, GROUP, 128), jnp.float32),
            pltpu.VMEM((3, 16, GROUP, 128), jnp.float32),
            pltpu.VMEM((ROWS, 2 * WT), bf16),
            pltpu.VMEM((ROWS, 2 * WR), bf16),
            pltpu.VMEM((ROWS, 2 * WT), bf16),
            pltpu.VMEM((ROWS, 2 * WR), bf16),
            pltpu.VMEM((ROWS, 2 * COLS), jnp.float32),
            pltpu.VMEM((ROWS, 2 * COLS), jnp.float32),
            pltpu.SemaphoreType.DMA((NZ, NA + 1)),
            pltpu.SemaphoreType.DMA((NZ, 4)),
        ],
        compiler_params=pltpu.CompilerParams(vmem_limit_bytes=54 * 2**20),
        name="heads",
    )(*operands)


def local(hidden_t, gain_t, head_t, hidden_r, gain_r, head_r):
    xl, y, core, z, xh = (lax.axis_index(name) for name in AXES)
    x = 2 * xh + xl

    head_r_other = send(head_r, other_core)
    head_t_other = send(head_t, other_core)
    second_r = jnp.concatenate([hidden_t[:, FA:], hidden_r], axis=1)[None]
    first_t = hidden_t[None, :, :FA]
    for x_core, step in ((0, 0), (0, 1), (1, 0)):
        got_r = send(second_r, pair_x_or_y(PAIRS4[step], x_core))
        got_t = send(first_t, pair_z(PAIRS8[2 * x_core + step]))
        second_r = jnp.concatenate([second_r, got_r])
        first_t = jnp.concatenate([first_t, got_t])
        second_r, first_t = lax.optimization_barrier((second_r, first_t))
    first_t = after(first_t, head_r_other, head_t_other)[None]
    before, behind = send(first_t, x_or_y(1, 1)), send(first_t, x_or_y(-1, 1))
    got_r = send(second_r, pair_x_or_y(PAIRS4[1], 1))
    second_r = jnp.concatenate([second_r, got_r])
    one_t = jnp.concatenate([first_t, before])
    one_t, before = lax.optimization_barrier((one_t, before, behind, got_r))[:2]
    two_t = jnp.concatenate([behind, send(before, x_or_y(1, 1))])
    blocks_c = ring8(second_r, core)
    low_one, high_one = send(one_t, x_or_y(1, 0)), send(one_t, x_or_y(-1, 0))
    ready_t = after(two_t, low_one, high_one, *blocks_c[1:3])
    low_two, high_two = send(ready_t, x_or_y(1, 0)), send(ready_t, x_or_y(-1, 0))
    far_one = send(after(low_one, low_two, high_two), x_or_y(1, 0))
    far_two = send(after(high_two, low_two), x_or_y(-1, 0))
    blocks_a = [one_t, two_t, low_one, low_two, high_one, high_two, far_one, far_two]

    ring = jnp.array((0, -1, 1, 2), jnp.int32)
    zeros = jnp.zeros((4, 4), jnp.int32)
    last, middle = zeros + ring[:, None], zeros + ring[None, :]
    on_x = core == 0
    xa = (x + jnp.where(on_x, last, middle)) % NX
    ya = (y + jnp.where(on_x, middle, last)) % NY
    in_x = zeros + jnp.where(on_x, jnp.array(sources(PAIRS4))[x][None, :], jnp.array(sources(PAIRS4))[x][:, None])
    in_y = zeros + jnp.where(on_x, jnp.array(sources(PAIRS4))[y][:, None], jnp.array(sources(PAIRS4))[y][None, :])
    xc, yc = in_x, in_y
    zs_c = (z + jnp.array(RING8, jnp.int32)) % NZ
    zs_a = jnp.array(sources(PAIRS8))[z]
    table = jnp.concatenate(
        [
            ((xa % 2) * NY + ya).reshape(16),
            (xa // 2).reshape(16),
            zs_c,
            ((xc % 2) * NY + yc).reshape(16),
            (xc // 2).reshape(16),
            jnp.argmax(zs_a[None, :] == zs_c[:, None], axis=1),
        ]
    ).astype(jnp.int32)

    wide_gain_t = gain_t.astype(jnp.float32).reshape(16, 1, WT)
    wide_gain_r = gain_r.astype(jnp.float32).reshape(16, 1, WR)
    logits, logits_cross, stats = heads_call(
        table,
        wide_gain_t, wide_gain_r,
        *blocks_a, *blocks_c,
        head_t.reshape(NZ, 2 * WT, COLS), head_t_other.reshape(NZ, 2 * WT, COLS),
        head_r.reshape(NZ, 2 * WR, COLS), head_r_other.reshape(NZ, 2 * WR, COLS),
    )

    logits_other = send(logits_cross, other_core)
    for pair, steps in ((pair_x, PAIRS4), (pair_y, PAIRS4), (pair_z, PAIRS8)):
        for partner in steps:
            stats = merge([stats, send(stats, pair(partner))])
    stats_other = send(stats, other_core)

    out = pl.pallas_call(
        contrast_kernel,
        out_shape=jax.ShapeDtypeStruct((8, 2, GROUP, COLS), jnp.float32),
        in_specs=[smem] + [vmem] * 4,
        out_specs=vmem,
        name="contrast",
    )(core.astype(jnp.int32).reshape(1), stats, stats_other, logits, logits_other)
    return out.reshape(2 * ROWS, COLS)


def solution(mesh):
    fine = Mesh(np.asarray(mesh.devices).reshape(SIZES), AXES)
    rows, features, vocabulary = ("xl", "y", "core"), ("z", "xh"), AXES
    placed = (
        P(rows, features),
        P(),
        P(None, vocabulary),
        P(rows, features),
        P(),
        P(None, vocabulary),
    )
    return jax.shard_map(
        local, mesh=fine, in_specs=placed, out_specs=P(None, vocabulary), check_vma=False
    )
```

```python
import functools

import jax
import jax.numpy as jnp
import numpy as np
from jax import lax
from jax.experimental import pallas as pl
from jax.experimental.pallas import tpu as pltpu
from jax.sharding import Mesh
from jax.sharding import PartitionSpec as P

EPS = 1e-05
LOG_TEN = 2.302585092994046

AXES = ("xl", "y", "core", "z", "xh")
SIZES = (2, 4, 2, 8, 2)
NX, NY, NZ = 4, 4, 8

D, DR = 16384, 4096
ROWS = 256
COLS = 256
GROUP = 32
WT, WR = 1024, 256
FA = 896
FC = WT - FA + WR
RING8 = (0, -1, 1, -2, 2, -3, 3, 4)


def flat_index(x, y, z, c):
    xl, xh = x % 2, x // 2
    return (((xl * NY + y) * 2 + c) * NZ + z) * 2 + xh


def send(value, move):
    pairs = []
    for xl, y, c, z, xh in np.ndindex(*SIZES):
        x = 2 * xh + xl
        tx, ty, tz, tc = move(x, y, z, c)
        pairs.append((flat_index(x, y, z, c), flat_index(tx % NX, ty % NY, tz % NZ, tc % 2)))
    return lax.ppermute(value, AXES, pairs)


PAIRS4 = ((1, 0, 3, 2), (3, 2, 1, 0))
PAIRS8 = ((1, 0, 3, 2, 5, 4, 7, 6), (7, 2, 1, 4, 3, 6, 5, 0), (3, 6, 5, 0, 7, 2, 1, 4))


def sources(pairs):
    rows = [[place] for place in range(len(pairs[0]))]
    for partner in pairs:
        rows = [rows[place] + rows[partner[place]] for place in range(len(rows))]
    return np.array(rows, np.int32)


def along_z(step):
    return lambda x, y, z, c: (x, y, z + step, c)


def pair_z(partner):
    return lambda x, y, z, c: (x, y, partner[z], c)


def pair_x(partner):
    return lambda x, y, z, c: (partner[x], y, z, c)


def pair_y(partner):
    return lambda x, y, z, c: (x, partner[y], z, c)


def pair_x_or_y(partner, x_core):
    return lambda x, y, z, c: (partner[x], y, z, c) if c == x_core else (x, partner[y], z, c)


def other_core(x, y, z, c):
    return (x, y, z, 1 - c)


def x_or_y(step, x_core):
    return lambda x, y, z, c: (x + step, y, z, c) if c == x_core else (x, y + step, z, c)


def after(value, *others):
    return lax.optimization_barrier((value,) + others)[0]


def ring8(value, core):
    low1 = send(value, along_z(1))
    high1 = send(value, along_z(-1))
    low2 = send(low1, along_z(1))
    high2 = send(high1, along_z(-1))
    low3 = send(low2, along_z(1))
    high3 = send(high2, along_z(-1))
    far = send(jnp.where(core == 0, low3, high3), lambda x, y, z, c: (x, y, z + 1 - 2 * c, c))
    return [value, low1, high1, low2, high2, low3, high3, far]


A_SLOTS = ((0, 0, 2), (0, 2, 2), (1, 0, 2), (1, 2, 2), (2, 0, 2), (2, 2, 2), (3, 0, 2), (3, 2, 2))
NA = len(A_SLOTS)
EARLY = NZ // 2


def head_copies(own, other, z, to, sems):
    return [
        pltpu.make_async_copy(own.at[z], to.at[0], sems.at[0]),
        pltpu.make_async_copy(other.at[z], to.at[1], sems.at[1]),
    ]


def preload_kernel(table_ref, own_ref, other_ref, to_ref, sems):
    copies = [
        copy
        for i in range(EARLY)
        for copy in head_copies(own_ref, other_ref, table_ref[32 + i], to_ref.at[i], sems.at[i])
    ]
    for copy in copies:
        copy.start()
    for copy in copies:
        copy.wait()


def preload(table, own, other):
    early = pl.pallas_call(
        preload_kernel,
        out_shape=pltpu.VMEM((EARLY, 2, 2 * WT, COLS), jnp.bfloat16),
        in_specs=[smem] + [hbm] * 2,
        out_specs=vmem,
        scratch_shapes=[pltpu.SemaphoreType.DMA((EARLY, 2))],
        compiler_params=pltpu.CompilerParams(vmem_limit_bytes=44 * 2**20),
        name="preload",
    )(table, own, other)
    return pltpu.with_memory_space_constraint(early, pltpu.VMEM)


def heads_kernel(*refs):
    table_ref, gain_t_ref, gain_r_ref = refs[:3]
    a_refs, c_refs, head_refs = refs[3 : 3 + NA], refs[3 + NA : 11 + NA], refs[11 + NA : 15 + NA]
    head_t_own, head_t_other, head_r_own, head_r_other = head_refs
    early_t = refs[15 + NA]
    logits_own, logits_cross, stats_ref = refs[16 + NA : 19 + NA]
    buf_a, buf_c, buf_t, buf_r = refs[19 + NA : 23 + NA]
    scale_t, scale_r, sums, left_t0, left_r0, left_t1, left_r1, sum_t, sum_r, sem_x, sem_t, sem_r = refs[23 + NA :]
    lefts = ((left_t0, left_r0), (left_t1, left_r1))

    def hidden_copies(i, c_ref):
        out = []
        place_a = table_ref[72 + i]
        for n, (ref, (k, j, count)) in enumerate(zip(a_refs, A_SLOTS)):
            target = buf_a.at[i, k, pl.ds(j, count)]
            out.append(pltpu.make_async_copy(ref.at[:, place_a], target, sem_x.at[i, n]))
        out.append(pltpu.make_async_copy(c_ref, buf_c.at[i], sem_x.at[i, NA]))
        return out

    early, late = [], []
    for i in range(NZ):
        z = table_ref[32 + i]
        wanted = early if i < EARLY else late
        wanted += head_copies(head_r_own, head_r_other, z, buf_r.at[i], sem_r.at[i])
        if i >= EARLY:
            at = i - EARLY
            wanted += head_copies(head_t_own, head_t_other, z, buf_t.at[at], sem_t.at[at])
    for i in range(NZ):
        for copy in hidden_copies(i, c_refs[i]):
            copy.start()
    for copy in early + late:
        copy.start()

    sums[...] = jnp.zeros_like(sums)

    def square_step(i, carry):
        for copy in hidden_copies(i, c_refs[0]):
            copy.wait()

        def lanes(ref, low, high):
            total = None
            for at in range(low, high, 128):
                part = ref[:, at : at + 128].astype(jnp.float32)
                total = part * part if total is None else total + part * part
            return total

        for n in range(16):
            sums[0, n] += lanes(buf_a.at[i, n // 4, n % 4], 0, FA)
            sums[1, n] += lanes(buf_c.at[i, n], 0, WT - FA)
            sums[2, n] += lanes(buf_c.at[i, n], WT - FA, FC)
        return carry

    lax.fori_loop(0, NZ, square_step, 0)
    scale_t[...] = jnp.zeros_like(scale_t)
    scale_r[...] = jnp.zeros_like(scale_r)
    for n in range(16):
        scale_t[table_ref[n]] += sums[0, n]
        scale_t[table_ref[40 + n]] += sums[1, n]
        scale_r[table_ref[40 + n]] += sums[2, n]
    for scale, width in ((scale_t, D), (scale_r, DR)):
        mean = jnp.sum(scale[...], axis=2, keepdims=True) * (1.0 / width)
        scale[...] = jnp.broadcast_to(lax.rsqrt(mean + EPS), scale.shape)

    def place(i, left):
        left_t, left_r = left
        z = table_ref[32 + i]

        def put(source, at, scale, group, gain, target, xh, column, width):
            rows = pl.ds(pl.multiple_of(group * GROUP, GROUP), GROUP)
            value = source[:, at : at + 128].astype(jnp.float32)
            value = value * scale[group] * gain[z * 2 + xh][:, column : column + 128]
            to = pl.ds(pl.multiple_of(xh * width + column, 128), 128)
            target[rows, to] = value.astype(jnp.bfloat16)

        for n in range(16):
            group, xh = table_ref[n], table_ref[16 + n]
            for at in range(0, FA, 128):
                put(buf_a.at[i, n // 4, n % 4], at, scale_t, group, gain_t_ref, left_t, xh, at, WT)
            group, xh = table_ref[40 + n], table_ref[56 + n]
            for at in range(0, WT - FA, 128):
                put(buf_c.at[i, n], at, scale_t, group, gain_t_ref, left_t, xh, FA + at, WT)
            for at in range(0, WR, 128):
                source = buf_c.at[i, n]
                put(source, WT - FA + at, scale_r, group, gain_r_ref, left_r, xh, at, WR)

    sum_t[...] = jnp.zeros_like(sum_t)
    sum_r[...] = jnp.zeros_like(sum_r)

    def multiply(i, left, heads_t, first):
        left_t, left_r = left
        for rows, heads, total in (
            (left_t, heads_t.at[i], sum_t),
            (left_r, buf_r.at[first + i], sum_r),
        ):
            for slot in range(2):
                at = pl.ds(slot * COLS, COLS)
                total[:, at] += jnp.dot(rows[...], heads[slot], preferred_element_type=jnp.float32)

    place(0, lefts[0])

    def steps(first, heads_t):
        def pair_step(pair, carry):
            i = pair * 2
            place(first + i + 1, lefts[1])
            multiply(i, lefts[0], heads_t, first)
            place(jnp.minimum(first + i + 2, NZ - 1), lefts[0])
            multiply(i + 1, lefts[1], heads_t, first)
            return carry

        lax.fori_loop(0, EARLY // 2, pair_step, 0)

    for copy in early:
        copy.wait()
    steps(0, early_t)
    for copy in late:
        copy.wait()
    steps(EARLY, buf_t)
    for model, total in enumerate((sum_t, sum_r)):
        logits_own[model] = total[:, :COLS]
        logits_cross[model] = total[:, COLS:]

    columns = []
    for model in range(2):
        one, two = logits_own[model], logits_cross[model]
        peak = jnp.max(jnp.maximum(one, two), axis=1, keepdims=True)
        total = jnp.sum(jnp.exp(one - peak) + jnp.exp(two - peak), axis=1, keepdims=True)
        columns.append((peak, total))
    lane = lax.broadcasted_iota(jnp.int32, (ROWS, 128), 1)
    packed = jnp.where(
        lane == 0,
        columns[0][0],
        jnp.where(lane == 1, columns[1][0], jnp.where(lane == 2, columns[0][1], columns[1][1])),
    )
    stats_ref[...] = packed.T[:8, :]


def contrast_kernel(core_ref, own_ref, other_ref, logits_own, logits_other, out_ref):
    core = core_ref[0]

    def score(stats, logits, where):
        logits_t, logits_r = logits[0], logits[1]
        tall = jnp.concatenate([stats, jnp.zeros((120, ROWS), jnp.float32)], axis=0).T
        peak_t, peak_r = tall[:, 0:1], tall[:, 1:2]
        lse_t = peak_t + jnp.log(tall[:, 2:3])
        lse_r = peak_r + jnp.log(tall[:, 3:4])
        margin = jnp.minimum(0.0, logits_t - peak_t + LOG_TEN)
        value = logits_t - lse_t - 0.5 * (logits_r - lse_r) + margin
        for group in range(ROWS // GROUP):
            out_ref[group, where] = value[group * GROUP : (group + 1) * GROUP]

    score(own_ref[...], logits_own, core)
    score(other_ref[...], logits_other, 1 - core)


def merge(parts):
    peaks = functools.reduce(jnp.maximum, [p[0:2] for p in parts])
    totals = sum(p[2:4] * jnp.exp(p[0:2] - peaks) for p in parts)
    return jnp.concatenate([peaks, totals, jnp.zeros_like(p8(parts[0]))], axis=0)


def p8(part):
    return part[4:8]


vmem = pl.BlockSpec(memory_space=pltpu.VMEM)
smem = pl.BlockSpec(memory_space=pltpu.SMEM)
hbm = pl.BlockSpec(memory_space=pl.ANY)


def heads_call(*operands):
    square = jax.ShapeDtypeStruct((2, ROWS, COLS), jnp.float32)
    bf16 = jnp.bfloat16
    return pl.pallas_call(
        heads_kernel,
        out_shape=[square] * 2 + [jax.ShapeDtypeStruct((8, ROWS), jnp.float32)],
        in_specs=[smem] + [vmem] * 2 + [hbm] * (NA + 12) + [vmem],
        out_specs=[vmem] * 3,
        scratch_shapes=[
            pltpu.VMEM((NZ, 4, 4, GROUP, FA), bf16),
            pltpu.VMEM((NZ, 16, GROUP, FC), bf16),
            pltpu.VMEM((NZ - EARLY, 2, 2 * WT, COLS), bf16),
            pltpu.VMEM((NZ, 2, 2 * WR, COLS), bf16),
            pltpu.VMEM((8, GROUP, 128), jnp.float32),
            pltpu.VMEM((8, GROUP, 128), jnp.float32),
            pltpu.VMEM((3, 16, GROUP, 128), jnp.float32),
            pltpu.VMEM((ROWS, 2 * WT), bf16),
            pltpu.VMEM((ROWS, 2 * WR), bf16),
            pltpu.VMEM((ROWS, 2 * WT), bf16),
            pltpu.VMEM((ROWS, 2 * WR), bf16),
            pltpu.VMEM((ROWS, 2 * COLS), jnp.float32),
            pltpu.VMEM((ROWS, 2 * COLS), jnp.float32),
            pltpu.SemaphoreType.DMA((NZ, NA + 1)),
            pltpu.SemaphoreType.DMA((NZ - EARLY, 2)),
            pltpu.SemaphoreType.DMA((NZ, 2)),
        ],
        compiler_params=pltpu.CompilerParams(vmem_limit_bytes=28 * 2**20),
        name="heads",
    )(*operands)


def local(hidden_t, gain_t, head_t, hidden_r, gain_r, head_r):
    xl, y, core, z, xh = (lax.axis_index(name) for name in AXES)
    x = 2 * xh + xl

    head_r_other = send(head_r, other_core)
    head_t_other = send(head_t, other_core)
    got_t = send(hidden_t[None], pair_z(PAIRS8[0]))[:, :, :FA]
    second_r = jnp.concatenate([hidden_t[:, FA:], hidden_r], axis=1)[None]
    got_r = send(second_r, pair_x_or_y(PAIRS4[0], 0))
    second_r = jnp.concatenate([second_r, got_r])
    first_t = jnp.concatenate([hidden_t[None, :, :FA], got_t])
    second_r, first_t = lax.optimization_barrier((second_r, first_t))
    got_t = send(first_t, pair_z(PAIRS8[1]))
    got_r = send(second_r, pair_x_or_y(PAIRS4[1], 0))
    second_r = jnp.concatenate([second_r, got_r])
    second_r, got_t = lax.optimization_barrier((second_r, got_t))
    near_t = send(got_t, pair_z(PAIRS8[0]))
    next_t = send(got_t, lambda x, y, z, c: (x, y, PAIRS8[1][PAIRS8[0][z]], c))
    got_r = send(second_r, pair_x_or_y(PAIRS4[0], 1))
    second_r = jnp.concatenate([second_r, got_r])
    first_t = jnp.concatenate([first_t, got_t, near_t, next_t])
    second_r, first_t = lax.optimization_barrier((second_r, first_t))
    first_t = after(first_t, head_r_other, head_t_other)[None]
    before, behind = send(first_t, x_or_y(1, 1)), send(first_t, x_or_y(-1, 1))
    got_r = send(second_r, pair_x_or_y(PAIRS4[1], 1))
    second_r = jnp.concatenate([second_r, got_r])
    one_t = jnp.concatenate([first_t, before])
    one_t, before = lax.optimization_barrier((one_t, before, behind, got_r))[:2]
    two_t = jnp.concatenate([behind, send(before, x_or_y(1, 1))])
    blocks_c = ring8(second_r, core)
    low_one, high_one = send(one_t, x_or_y(1, 0)), send(one_t, x_or_y(-1, 0))
    ready_t = after(two_t, low_one, high_one, *blocks_c[1:3])
    low_two, high_two = send(ready_t, x_or_y(1, 0)), send(ready_t, x_or_y(-1, 0))
    far_one = send(after(low_one, low_two, high_two), x_or_y(1, 0))
    far_two = send(after(high_two, low_two), x_or_y(-1, 0))
    blocks_a = [one_t, two_t, low_one, low_two, high_one, high_two, far_one, far_two]

    ring = jnp.array((0, -1, 1, 2), jnp.int32)
    zeros = jnp.zeros((4, 4), jnp.int32)
    last, middle = zeros + ring[:, None], zeros + ring[None, :]
    on_x = core == 0
    xa = (x + jnp.where(on_x, last, middle)) % NX
    ya = (y + jnp.where(on_x, middle, last)) % NY
    in_x = zeros + jnp.where(on_x, jnp.array(sources(PAIRS4))[x][None, :], jnp.array(sources(PAIRS4))[x][:, None])
    in_y = zeros + jnp.where(on_x, jnp.array(sources(PAIRS4))[y][:, None], jnp.array(sources(PAIRS4))[y][None, :])
    xc, yc = in_x, in_y
    zs_c = (z + jnp.array(RING8, jnp.int32)) % NZ
    one, two = (np.array(pairs) for pairs in PAIRS8[:2])
    starts = [np.arange(NZ), two, two[one], two[one[two]]]
    zs_a = jnp.array(np.stack([v for at in starts for v in (at, one[at])], axis=1), jnp.int32)[z]
    table = jnp.concatenate(
        [
            ((xa % 2) * NY + ya).reshape(16),
            (xa // 2).reshape(16),
            zs_c,
            ((xc % 2) * NY + yc).reshape(16),
            (xc // 2).reshape(16),
            jnp.argmax(zs_a[None, :] == zs_c[:, None], axis=1),
        ]
    ).astype(jnp.int32)

    heads = [head.reshape(NZ, -1, COLS) for head in (head_t, head_t_other, head_r, head_r_other)]
    early = preload(table, *heads[:2])
    wide_gain_t = gain_t.astype(jnp.float32).reshape(16, 1, WT)
    wide_gain_r = gain_r.astype(jnp.float32).reshape(16, 1, WR)
    logits, logits_cross, stats = heads_call(
        table,
        wide_gain_t, wide_gain_r,
        *blocks_a, *blocks_c,
        *heads, early,
    )

    logits_other = send(logits_cross, other_core)
    for pair, steps in ((pair_x, PAIRS4), (pair_y, PAIRS4), (pair_z, PAIRS8)):
        for partner in steps:
            stats = merge([stats, send(stats, pair(partner))])
    stats_other = send(stats, other_core)

    out = pl.pallas_call(
        contrast_kernel,
        out_shape=jax.ShapeDtypeStruct((8, 2, GROUP, COLS), jnp.float32),
        in_specs=[smem] + [vmem] * 4,
        out_specs=vmem,
        name="contrast",
    )(core.astype(jnp.int32).reshape(1), stats, stats_other, logits, logits_other)
    return out.reshape(2 * ROWS, COLS)


def solution(mesh):
    fine = Mesh(np.asarray(mesh.devices).reshape(SIZES), AXES)
    rows, features, vocabulary = ("xl", "y", "core"), ("z", "xh"), AXES
    placed = (
        P(rows, features),
        P(),
        P(None, vocabulary),
        P(rows, features),
        P(),
        P(None, vocabulary),
    )
    return jax.shard_map(
        local, mesh=fine, in_specs=placed, out_specs=P(None, vocabulary), check_vma=False
    )
```

```python
import functools

import jax
import jax.numpy as jnp
import numpy as np
from jax import lax
from jax.experimental import pallas as pl
from jax.experimental.pallas import tpu as pltpu
from jax.sharding import Mesh
from jax.sharding import PartitionSpec as P

EPS = 1e-05
LOG_TEN = 2.302585092994046

AXES = ("xl", "y", "core", "z", "xh")
SIZES = (2, 4, 2, 8, 2)
NX, NY, NZ = 4, 4, 8

D, DR = 16384, 4096
ROWS = 256
COLS = 256
GROUP = 32
WT, WR = 1024, 256
FA = 896
FC = WT - FA + WR
RING8 = (0, -1, 1, -2, 2, -3, 3, 4)


def flat_index(x, y, z, c):
    xl, xh = x % 2, x // 2
    return (((xl * NY + y) * 2 + c) * NZ + z) * 2 + xh


def send(value, move):
    pairs = []
    for xl, y, c, z, xh in np.ndindex(*SIZES):
        x = 2 * xh + xl
        tx, ty, tz, tc = move(x, y, z, c)
        pairs.append((flat_index(x, y, z, c), flat_index(tx % NX, ty % NY, tz % NZ, tc % 2)))
    return lax.ppermute(value, AXES, pairs)


PAIRS4 = ((1, 0, 3, 2), (3, 2, 1, 0))
PAIRS8 = ((1, 0, 3, 2, 5, 4, 7, 6), (7, 2, 1, 4, 3, 6, 5, 0), (3, 6, 5, 0, 7, 2, 1, 4))


def sources(pairs):
    rows = [[place] for place in range(len(pairs[0]))]
    for partner in pairs:
        rows = [rows[place] + rows[partner[place]] for place in range(len(rows))]
    return np.array(rows, np.int32)


def along_z(step):
    return lambda x, y, z, c: (x, y, z + step, c)


def pair_z(partner):
    return lambda x, y, z, c: (x, y, partner[z], c)


def pair_x(partner):
    return lambda x, y, z, c: (partner[x], y, z, c)


def pair_y(partner):
    return lambda x, y, z, c: (x, partner[y], z, c)


def pair_x_or_y(partner, x_core):
    return lambda x, y, z, c: (partner[x], y, z, c) if c == x_core else (x, partner[y], z, c)


def other_core(x, y, z, c):
    return (x, y, z, 1 - c)


def x_or_y(step, x_core):
    return lambda x, y, z, c: (x + step, y, z, c) if c == x_core else (x, y + step, z, c)


def after(value, *others):
    return lax.optimization_barrier((value,) + others)[0]


def ring8(value, core):
    low1 = send(value, along_z(1))
    high1 = send(value, along_z(-1))
    low2 = send(low1, along_z(1))
    high2 = send(high1, along_z(-1))
    low3 = send(low2, along_z(1))
    high3 = send(high2, along_z(-1))
    far = send(jnp.where(core == 0, low3, high3), lambda x, y, z, c: (x, y, z + 1 - 2 * c, c))
    return [value, low1, high1, low2, high2, low3, high3, far]


A_SLOTS = ((0, 0, 2), (0, 2, 2), (1, 0, 2), (1, 2, 2), (2, 0, 2), (2, 2, 2), (3, 0, 2), (3, 2, 2))
NA = len(A_SLOTS)
EARLY = NZ // 2


def head_copies(own, other, z, to, sems):
    return [
        pltpu.make_async_copy(own.at[z], to.at[0], sems.at[0]),
        pltpu.make_async_copy(other.at[z], to.at[1], sems.at[1]),
    ]


def preload_kernel(table_ref, own_ref, other_ref, to_ref, sems):
    copies = [
        copy
        for i in range(EARLY)
        for copy in head_copies(own_ref, other_ref, table_ref[32 + i], to_ref.at[i], sems.at[i])
    ]
    for copy in copies:
        copy.start()
    for copy in copies:
        copy.wait()


def preload(table, own, other):
    early = pl.pallas_call(
        preload_kernel,
        out_shape=pltpu.VMEM((EARLY, 2, 2 * WT, COLS), jnp.bfloat16),
        in_specs=[smem] + [hbm] * 2,
        out_specs=vmem,
        scratch_shapes=[pltpu.SemaphoreType.DMA((EARLY, 2))],
        compiler_params=pltpu.CompilerParams(vmem_limit_bytes=44 * 2**20),
        name="preload",
    )(table, own, other)
    return pltpu.with_memory_space_constraint(early, pltpu.VMEM)


def heads_kernel(*refs):
    table_ref, gain_t_ref, gain_r_ref = refs[:3]
    a_refs, c_refs, head_refs = refs[3 : 3 + NA], refs[3 + NA : 11 + NA], refs[11 + NA : 15 + NA]
    head_t_own, head_t_other, head_r_own, head_r_other = head_refs
    early_t = refs[15 + NA]
    logits_own, logits_cross, stats_ref = refs[16 + NA : 19 + NA]
    buf_a, buf_c, buf_t, buf_r = refs[19 + NA : 23 + NA]
    scale_t, scale_r, sums, left_t0, left_r0, left_t1, left_r1, sum_t, sum_r, sem_x, sem_t, sem_r = refs[23 + NA :]
    lefts = ((left_t0, left_r0), (left_t1, left_r1))

    def hidden_copies(i, c_ref):
        out = []
        place_a = table_ref[72 + i]
        for n, (ref, (k, j, count)) in enumerate(zip(a_refs, A_SLOTS)):
            target = buf_a.at[i, k, pl.ds(j, count)]
            out.append(pltpu.make_async_copy(ref.at[:, place_a], target, sem_x.at[i, n]))
        out.append(pltpu.make_async_copy(c_ref, buf_c.at[i], sem_x.at[i, NA]))
        return out

    early, late = [], []
    for i in range(NZ):
        z = table_ref[32 + i]
        wanted = early if i < EARLY else late
        wanted += head_copies(head_r_own, head_r_other, z, buf_r.at[i], sem_r.at[i])
        if i >= EARLY:
            at = i - EARLY
            wanted += head_copies(head_t_own, head_t_other, z, buf_t.at[at], sem_t.at[at])
    for i in range(NZ):
        for copy in hidden_copies(i, c_refs[i]):
            copy.start()
    for copy in early + late:
        copy.start()

    sums[...] = jnp.zeros_like(sums)

    def square_step(i, carry):
        for copy in hidden_copies(i, c_refs[0]):
            copy.wait()

        def lanes(ref, low, high):
            total = None
            for at in range(low, high, 128):
                part = ref[:, at : at + 128].astype(jnp.float32)
                total = part * part if total is None else total + part * part
            return total

        for n in range(16):
            sums[0, n] += lanes(buf_a.at[i, n // 4, n % 4], 0, FA)
            sums[1, n] += lanes(buf_c.at[i, n], 0, WT - FA)
            sums[2, n] += lanes(buf_c.at[i, n], WT - FA, FC)
        return carry

    lax.fori_loop(0, NZ, square_step, 0)
    scale_t[...] = jnp.zeros_like(scale_t)
    scale_r[...] = jnp.zeros_like(scale_r)
    for n in range(16):
        scale_t[table_ref[n]] += sums[0, n]
        scale_t[table_ref[40 + n]] += sums[1, n]
        scale_r[table_ref[40 + n]] += sums[2, n]
    for scale, width in ((scale_t, D), (scale_r, DR)):
        mean = jnp.sum(scale[...], axis=2, keepdims=True) * (1.0 / width)
        scale[...] = jnp.broadcast_to(lax.rsqrt(mean + EPS), scale.shape)

    def place(i, left):
        left_t, left_r = left
        z = table_ref[32 + i]

        def put(source, at, scale, group, gain, target, xh, column, width):
            rows = pl.ds(pl.multiple_of(group * GROUP, GROUP), GROUP)
            value = source[:, at : at + 128].astype(jnp.float32)
            value = value * scale[group] * gain[z * 2 + xh][:, column : column + 128]
            to = pl.ds(pl.multiple_of(xh * width + column, 128), 128)
            target[rows, to] = value.astype(jnp.bfloat16)

        for n in range(16):
            group, xh = table_ref[n], table_ref[16 + n]
            for at in range(0, FA, 128):
                put(buf_a.at[i, n // 4, n % 4], at, scale_t, group, gain_t_ref, left_t, xh, at, WT)
            group, xh = table_ref[40 + n], table_ref[56 + n]
            for at in range(0, WT - FA, 128):
                put(buf_c.at[i, n], at, scale_t, group, gain_t_ref, left_t, xh, FA + at, WT)
            for at in range(0, WR, 128):
                source = buf_c.at[i, n]
                put(source, WT - FA + at, scale_r, group, gain_r_ref, left_r, xh, at, WR)

    sum_t[...] = jnp.zeros_like(sum_t)
    sum_r[...] = jnp.zeros_like(sum_r)

    def multiply(i, left, heads_t, first):
        left_t, left_r = left
        for rows, heads, total in (
            (left_t, heads_t.at[i], sum_t),
            (left_r, buf_r.at[first + i], sum_r),
        ):
            for slot in range(2):
                at = pl.ds(slot * COLS, COLS)
                total[:, at] += jnp.dot(rows[...], heads[slot], preferred_element_type=jnp.float32)

    place(0, lefts[0])

    def steps(first, heads_t):
        def pair_step(pair, carry):
            i = pair * 2
            place(first + i + 1, lefts[1])
            multiply(i, lefts[0], heads_t, first)
            place(jnp.minimum(first + i + 2, NZ - 1), lefts[0])
            multiply(i + 1, lefts[1], heads_t, first)
            return carry

        lax.fori_loop(0, EARLY // 2, pair_step, 0)

    for copy in early:
        copy.wait()
    steps(0, early_t)
    for copy in late:
        copy.wait()
    steps(EARLY, buf_t)
    for model, total in enumerate((sum_t, sum_r)):
        logits_own[model] = total[:, :COLS]
        logits_cross[model] = total[:, COLS:]

    columns = []
    for model in range(2):
        one, two = logits_own[model], logits_cross[model]
        peak = jnp.max(jnp.maximum(one, two), axis=1, keepdims=True)
        total = jnp.sum(jnp.exp(one - peak) + jnp.exp(two - peak), axis=1, keepdims=True)
        columns.append((peak, total))
    lane = lax.broadcasted_iota(jnp.int32, (ROWS, 128), 1)
    packed = jnp.where(
        lane == 0,
        columns[0][0],
        jnp.where(lane == 1, columns[1][0], jnp.where(lane == 2, columns[0][1], columns[1][1])),
    )
    stats_ref[...] = packed.T[:8, :]


def contrast_kernel(core_ref, own_ref, other_ref, logits_own, logits_other, out_ref):
    core = core_ref[0]

    def score(stats, logits, where):
        logits_t, logits_r = logits[0], logits[1]
        tall = jnp.concatenate([stats, jnp.zeros((120, ROWS), jnp.float32)], axis=0).T
        peak_t, peak_r = tall[:, 0:1], tall[:, 1:2]
        lse_t = peak_t + jnp.log(tall[:, 2:3])
        lse_r = peak_r + jnp.log(tall[:, 3:4])
        margin = jnp.minimum(0.0, logits_t - peak_t + LOG_TEN)
        value = logits_t - lse_t - 0.5 * (logits_r - lse_r) + margin
        for group in range(ROWS // GROUP):
            out_ref[group, where] = value[group * GROUP : (group + 1) * GROUP]

    score(own_ref[...], logits_own, core)
    score(other_ref[...], logits_other, 1 - core)


def merge(parts):
    peaks = functools.reduce(jnp.maximum, [p[0:2] for p in parts])
    totals = sum(p[2:4] * jnp.exp(p[0:2] - peaks) for p in parts)
    return jnp.concatenate([peaks, totals, jnp.zeros_like(p8(parts[0]))], axis=0)


def p8(part):
    return part[4:8]


vmem = pl.BlockSpec(memory_space=pltpu.VMEM)
smem = pl.BlockSpec(memory_space=pltpu.SMEM)
hbm = pl.BlockSpec(memory_space=pl.ANY)


def heads_call(*operands):
    square = jax.ShapeDtypeStruct((2, ROWS, COLS), jnp.float32)
    bf16 = jnp.bfloat16
    return pl.pallas_call(
        heads_kernel,
        out_shape=[square] * 2 + [jax.ShapeDtypeStruct((8, ROWS), jnp.float32)],
        in_specs=[smem] + [vmem] * 2 + [hbm] * (NA + 12) + [vmem],
        out_specs=[vmem] * 3,
        scratch_shapes=[
            pltpu.VMEM((NZ, 4, 4, GROUP, FA), bf16),
            pltpu.VMEM((NZ, 16, GROUP, FC), bf16),
            pltpu.VMEM((NZ - EARLY, 2, 2 * WT, COLS), bf16),
            pltpu.VMEM((NZ, 2, 2 * WR, COLS), bf16),
            pltpu.VMEM((8, GROUP, 128), jnp.float32),
            pltpu.VMEM((8, GROUP, 128), jnp.float32),
            pltpu.VMEM((3, 16, GROUP, 128), jnp.float32),
            pltpu.VMEM((ROWS, 2 * WT), bf16),
            pltpu.VMEM((ROWS, 2 * WR), bf16),
            pltpu.VMEM((ROWS, 2 * WT), bf16),
            pltpu.VMEM((ROWS, 2 * WR), bf16),
            pltpu.VMEM((ROWS, 2 * COLS), jnp.float32),
            pltpu.VMEM((ROWS, 2 * COLS), jnp.float32),
            pltpu.SemaphoreType.DMA((NZ, NA + 1)),
            pltpu.SemaphoreType.DMA((NZ - EARLY, 2)),
            pltpu.SemaphoreType.DMA((NZ, 2)),
        ],
        compiler_params=pltpu.CompilerParams(vmem_limit_bytes=28 * 2**20),
        name="heads",
    )(*operands)


def local(hidden_t, gain_t, head_t, hidden_r, gain_r, head_r):
    xl, y, core, z, xh = (lax.axis_index(name) for name in AXES)
    x = 2 * xh + xl

    head_r_other = send(head_r, other_core)
    head_t_other = send(head_t, other_core)
    got_t = send(hidden_t[None], pair_z(PAIRS8[0]))[:, :, :FA]
    second_r = jnp.concatenate([hidden_t[:, FA:], hidden_r], axis=1)[None]
    got_r = send(second_r, pair_x_or_y(PAIRS4[0], 0))
    second_r = jnp.concatenate([second_r, got_r])
    first_t = jnp.concatenate([hidden_t[None, :, :FA], got_t])
    second_r, first_t = lax.optimization_barrier((second_r, first_t))
    got_t = send(first_t, pair_z(PAIRS8[1]))
    got_r = send(second_r, pair_x_or_y(PAIRS4[1], 0))
    second_r = jnp.concatenate([second_r, got_r])
    second_r, got_t = lax.optimization_barrier((second_r, got_t))
    near_t = send(got_t, pair_z(PAIRS8[0]))
    next_t = send(got_t, lambda x, y, z, c: (x, y, PAIRS8[1][PAIRS8[0][z]], c))
    got_r = send(second_r, pair_x_or_y(PAIRS4[0], 1))
    second_r = jnp.concatenate([second_r, got_r])
    first_t = jnp.concatenate([first_t, got_t, near_t, next_t])
    second_r, first_t = lax.optimization_barrier((second_r, first_t))
    first_t = after(first_t, head_r_other, head_t_other)[None]
    before, behind = send(first_t, x_or_y(1, 1)), send(first_t, x_or_y(-1, 1))
    got_r = send(second_r, pair_x_or_y(PAIRS4[1], 1))
    second_r = jnp.concatenate([second_r, got_r])
    one_t = jnp.concatenate([first_t, before])
    one_t, before = lax.optimization_barrier((one_t, before, behind, got_r))[:2]
    two_t = jnp.concatenate([behind, send(before, x_or_y(1, 1))])
    blocks_c = ring8(second_r, core)
    low_one, high_one = send(one_t, x_or_y(1, 0)), send(one_t, x_or_y(-1, 0))
    ready_t = after(two_t, low_one, high_one, *blocks_c[1:3])
    low_two, high_two = send(ready_t, x_or_y(1, 0)), send(ready_t, x_or_y(-1, 0))
    far_one = send(after(low_one, low_two, high_two), x_or_y(1, 0))
    far_two = send(after(high_two, low_two), x_or_y(-1, 0))
    blocks_a = [one_t, two_t, low_one, low_two, high_one, high_two, far_one, far_two]

    ring = jnp.array((0, -1, 1, 2), jnp.int32)
    zeros = jnp.zeros((4, 4), jnp.int32)
    last, middle = zeros + ring[:, None], zeros + ring[None, :]
    on_x = core == 0
    xa = (x + jnp.where(on_x, last, middle)) % NX
    ya = (y + jnp.where(on_x, middle, last)) % NY
    in_x = zeros + jnp.where(on_x, jnp.array(sources(PAIRS4))[x][None, :], jnp.array(sources(PAIRS4))[x][:, None])
    in_y = zeros + jnp.where(on_x, jnp.array(sources(PAIRS4))[y][:, None], jnp.array(sources(PAIRS4))[y][None, :])
    xc, yc = in_x, in_y
    zs_c = (z + jnp.array(RING8, jnp.int32)) % NZ
    one, two = (np.array(pairs) for pairs in PAIRS8[:2])
    starts = [np.arange(NZ), two, two[one], two[one[two]]]
    zs_a = jnp.array(np.stack([v for at in starts for v in (at, one[at])], axis=1), jnp.int32)[z]
    table = jnp.concatenate(
        [
            ((xa % 2) * NY + ya).reshape(16),
            (xa // 2).reshape(16),
            zs_c,
            ((xc % 2) * NY + yc).reshape(16),
            (xc // 2).reshape(16),
            jnp.argmax(zs_a[None, :] == zs_c[:, None], axis=1),
        ]
    ).astype(jnp.int32)

    heads = [head.reshape(NZ, -1, COLS) for head in (head_t, head_t_other, head_r, head_r_other)]
    early = preload(table, *heads[:2])
    wide_gain_t = gain_t.astype(jnp.float32).reshape(16, 1, WT)
    wide_gain_r = gain_r.astype(jnp.float32).reshape(16, 1, WR)
    logits, logits_cross, stats = heads_call(
        table,
        wide_gain_t, wide_gain_r,
        *blocks_a, *blocks_c,
        *heads, early,
    )

    logits_other = send(logits_cross, other_core)
    for pair, steps in ((pair_x, PAIRS4), (pair_y, PAIRS4), (pair_z, PAIRS8)):
        for partner in steps:
            stats = merge([stats, send(stats, pair(partner))])
    stats_other = send(stats, other_core)

    out = pl.pallas_call(
        contrast_kernel,
        out_shape=jax.ShapeDtypeStruct((8, 2, GROUP, COLS), jnp.float32),
        in_specs=[smem] + [vmem] * 4,
        out_specs=vmem,
        compiler_params=pltpu.CompilerParams(vmem_limit_bytes=8 * 2**20),
        name="contrast",
    )(
        core.astype(jnp.int32).reshape(1),
        *(
            pltpu.with_memory_space_constraint(value, pltpu.VMEM)
            for value in (stats, stats_other, logits, logits_other)
        ),
    )
    return out.reshape(2 * ROWS, COLS)


def solution(mesh):
    fine = Mesh(np.asarray(mesh.devices).reshape(SIZES), AXES)
    rows, features, vocabulary = ("xl", "y", "core"), ("z", "xh"), AXES
    placed = (
        P(rows, features),
        P(),
        P(None, vocabulary),
        P(rows, features),
        P(),
        P(None, vocabulary),
    )
    return jax.shard_map(
        local, mesh=fine, in_specs=placed, out_specs=P(None, vocabulary), check_vma=False
    )
```
